32 devices in a mesh: arc: 8 (over y, x, core), par: 4 (over z).
Axes of the slice: x: 2, y: 2, z: 4, core: 2. Of those that a mesh axis runs over, the one named last changes fastest.
Arguments:
- partials: bfloat16 [8, 3, 128, 8192], P('arc', None, 'par'), may hold values from -6 to 6
- epoch_index: int32 [8, 128], P('arc'), may hold values from 0 to 511, as said below
- whitening: float32 [8, 3, 128, 128], P('arc'), may hold values from -2 to 2, as said below
Outputs:
- normal_matrix: float32 [8192, 8192], P('arc', 'par')
The draws below stay inside these ranges and needn't reach their ends.
Inputs may be any that keep to these rules, and one draw needn't show every extreme that they name: `epoch_index`: in each arc the epoch indices rise strictly; the first is 0 and the last is 511. `whitening`: each block is lower triangular with diagonal entries between 1 and 2.
All inputs are finite; a program needn't handle non-finite values.
Results may differ from the reference program's by a relative error of at most 0.0003.
Values may be sent and summed in bfloat16 or wider, within the bound.
No kernel may reach another device: no remote copies, remote signals or barrier semaphores. Data moves between devices by JAX's collectives and lax.ppermute only.
A program may use at most 128 MiB of HBM per device.

```python
import math
import jax
import jax.numpy as jnp
from jax import lax

P_SIZE = 8192
E = 128
ARCS = 8


def draw_epoch_index(key, part):
    epoch_span = 4 * E
    arc_keys = jax.random.split(jax.random.fold_in(key, 5), ARCS)

    def per_arc(arc_key):
        interior = jnp.sort(jax.random.permutation(arc_key, epoch_span - 2)[:E - 2]) + 1
        first_one = jnp.zeros((1,), jnp.int32)
        last_one = jnp.full((1,), epoch_span - 1, jnp.int32)
        return jnp.concatenate([first_one, interior.astype(jnp.int32), last_one])
    return jax.vmap(per_arc)(arc_keys)


def draw_whitening(key, part):
    first_key, second_key = jax.random.split(jax.random.fold_in(key, 11))
    diagonal = jax.random.uniform(first_key, (ARCS, 3, E), jnp.float32, 1.0, 2.0)
    lower_part = jax.random.normal(second_key, (ARCS, 3, E, E), jnp.float32) * (0.6 / math.sqrt(E))
    lower_part = jnp.tril(lower_part, -1)
    return lower_part + diagonal[..., None] * jnp.eye(E, dtype=jnp.float32)


def block_levels(key, dims, cuts, least, largest):
    gain = 1.0
    for position, shards_of in cuts:
        draws = jax.random.uniform(jax.random.fold_in(jax.random.fold_in(key, 6), position), (shards_of,), jnp.float32, least / len(cuts), largest / len(cuts))
        gain = gain * jnp.repeat(jnp.exp(draws), dims[position] // shards_of).reshape((-1,) + (1,) * (len(dims) - 1 - position))
    return gain


def scatter_about(own_key, extent, spread, bound, shards=(), kind=jnp.bfloat16):
    result = jax.random.normal(own_key, extent, jnp.float32) * spread
    if len(shards) > 0:
        result = block_levels(own_key, extent, shards, -0.22, 0.18) * result
    return jnp.clip(result, min=-bound, max=bound).astype(kind)


def setup_inputs(seed: int = 0) -> dict:
    keys = jax.random.split(jax.random.key(seed), 4)
    partials = scatter_about(keys[0], (ARCS, 3, E, P_SIZE), 1.0, 6.0, ((0, 8), (2, 4)))
    epoch_index = draw_epoch_index(jax.random.fold_in(keys[3], 71), 0)
    whitening = draw_whitening(jax.random.fold_in(keys[3], 71), 0)
    return dict(partials=partials, epoch_index=epoch_index, whitening=whitening)


KERNEL_GAIN = 8.0

def mixing_matrices(epoch_index, whitening, epochs, row_scale):
    times_arc = epoch_index.astype(jnp.float32) / jnp.float32(4 * epochs - 1)
    later_time = times_arc[:, :, None]
    earlier_time = times_arc[:, None, :]
    green_part = jnp.minimum(later_time, earlier_time) * (1.0 - jnp.maximum(later_time, earlier_time))
    kernel = jnp.eye(epochs, dtype=jnp.float32)[None] + KERNEL_GAIN / epochs * green_part
    mixing = jnp.einsum('acij,ajk->acik', whitening, kernel, precision=lax.Precision.HIGHEST)
    return mixing * row_scale

def reference(partials, epoch_index, whitening):
    row_scale = 1.0 / math.sqrt(3 * E * ARCS)
    mixing = mixing_matrices(epoch_index, whitening, E, row_scale)
    panels = jnp.einsum('acij,acjk->acik', mixing, partials.astype(jnp.float32), precision=lax.Precision.HIGHEST)
    stacked = panels.reshape(-1, P_SIZE)
    return lax.dot_general(stacked, stacked, (((0,), (0,)), ((), ())), precision=lax.Precision.HIGHEST, preferred_element_type=jnp.float32)
```

```python
import math

import jax
import jax.numpy as jnp
from jax import lax
from jax.sharding import PartitionSpec as P

KERNEL_GAIN = 8.0


def mixing_matrices(epoch_index, whitening, epochs, row_scale):
    times_arc = epoch_index.astype(jnp.float32) / jnp.float32(4 * epochs - 1)
    later_time = times_arc[:, :, None]
    earlier_time = times_arc[:, None, :]
    green_part = jnp.minimum(later_time, earlier_time) * (
        1.0 - jnp.maximum(later_time, earlier_time)
    )
    kernel = jnp.eye(epochs, dtype=jnp.float32)[None] + KERNEL_GAIN / epochs * green_part
    mixing = jnp.einsum("acij,ajk->acik", whitening, kernel, precision=lax.Precision.HIGHEST)
    return mixing * row_scale


def gram_matrices(mixing):
    return jnp.einsum("acki,ackj->acij", mixing, mixing, precision=lax.Precision.HIGHEST)


def halves(value):
    high = lax.reduce_precision(value, 8, 7)
    return high.astype(jnp.bfloat16), (value - high).astype(jnp.bfloat16)


def mixed_rows(gram, rows):
    high, low = halves(gram)
    both = jnp.concatenate([high, low], axis=1)
    out = jnp.einsum("aij,ajn->ain", both, rows, preferred_element_type=jnp.float32)
    epochs = gram.shape[1]
    return halves(out[:, :epochs] + out[:, epochs:])


def product(rows, columns):
    contract = (((0, 1), (0, 1)), ((), ()))
    return sum(
        lax.dot_general(part, columns, contract, preferred_element_type=jnp.float32)
        for part in rows
    )


def general_on_device(partials, epoch_index, whitening):
    arc_local = partials.shape[0]
    epochs = epoch_index.shape[1]
    param_count = partials.shape[3]
    arc_count = lax.axis_size("arc")
    par_count = lax.axis_size("par")
    row_block = param_count // arc_count
    col_block = param_count // par_count
    row_scale = 1.0 / math.sqrt(3 * epochs * arc_local * arc_count)
    gram = gram_matrices(mixing_matrices(epoch_index, whitening, epochs, row_scale))
    gram = lax.all_gather(gram, "arc", axis=0, tiled=True)
    rows = lax.all_to_all(partials, "arc", split_axis=3, concat_axis=0, tiled=True)
    rows = lax.all_gather(rows, "par", axis=2, tiled=True)
    columns = lax.all_to_all(partials, "par", split_axis=3, concat_axis=2, tiled=True)
    columns = lax.all_gather(columns, "arc", axis=0, tiled=True)
    mixed = mixed_rows(gram.reshape(-1, epochs, epochs), rows.reshape(-1, epochs, row_block))
    return product(mixed, columns.reshape(-1, epochs, col_block))


def on_device(partials, epoch_index, whitening):
    arc_local, components, epoch_block, param_count = partials.shape
    epochs = epoch_index.shape[1]
    arc_count = lax.axis_size("arc")
    par_count = lax.axis_size("par")
    row_block = param_count // arc_count
    col_block = param_count // par_count
    total_arcs = arc_local * arc_count
    row_scale = 1.0 / math.sqrt(3 * epochs * total_arcs)
    z = lax.axis_index("par")
    bottom = z == 0
    top = z == par_count - 1
    at_end = bottom | top

    first = jnp.where(bottom, 1, z - 1)
    second = jnp.where(bottom, 2, jnp.where(top, z - 2, z + 1))
    third = jnp.where(bottom, 3, jnp.where(top, z - 3, jnp.where(z == 1, 3, 0)))
    order = jnp.stack([z, first, second, third])
    mixing = mixing_matrices(epoch_index, whitening, epochs, row_scale)
    mixing = mixing.reshape(arc_local, components, epochs, par_count, epoch_block)
    mixing = jnp.take(mixing, order, axis=3).reshape(arc_local, components, epochs, epochs)
    gram = lax.all_gather(gram_matrices(mixing), "arc", axis=0, tiled=True)

    def along(pairs):
        return lambda v: lax.ppermute(v, "par", pairs)

    up1, up2, up3 = along([(0, 1), (1, 2), (2, 3)]), along([(1, 2), (2, 3)]), along([(2, 3)])
    down1, down2, down3 = along([(3, 2), (2, 1), (1, 0)]), along([(2, 1), (1, 0)]), along([(1, 0)])

    def to_rows(block):
        parts = [block[:, i * row_block : (i + 1) * row_block] for i in range(arc_count)]
        parts = lax.optimization_barrier(jnp.stack(parts))
        return lax.all_to_all(parts, "arc", split_axis=0, concat_axis=0, tiled=True)

    def to_columns(block):
        part = lax.dynamic_slice_in_dim(block, z * col_block, col_block, 1)
        part = lax.optimization_barrier(part)
        return lax.all_gather(part, "arc", axis=0)

    total = 0.0
    own = partials.reshape(components * epoch_block, param_count)
    own_rows = to_rows(own)
    own_columns = to_columns(own)
    for c in range(components):
        here = slice(c * epoch_block, (c + 1) * epoch_block)
        raw = own[here]
        u1, d1 = up1(raw), down1(raw)
        u2, d2 = up2(u1), down2(d1)
        u3, d3 = up3(u2), down3(d2)
        f2 = jnp.where(z >= 2, u2, d2)
        g = [
            jnp.where(bottom, d1, u1),
            jnp.where(at_end, f2, d1),
            jnp.where(bottom, d3, jnp.where(top, u3, f2)),
        ]
        g = lax.optimization_barrier(jnp.concatenate(g, axis=0))
        rows = jnp.concatenate([own_rows[:, here], to_rows(g)], axis=1)
        columns = jnp.concatenate([own_columns[:, here], to_columns(g)], axis=1)
        columns = lax.optimization_barrier(columns)
        mixed = lax.optimization_barrier(mixed_rows(gram[:, c], rows))
        total = total + product(mixed, columns)
    return total


def solution(mesh):
    placed = (P("arc", None, "par", None), P("arc", None), P("arc", None, None, None))
    special = mesh.shape["par"] == 4 and mesh.shape["arc"] == 8
    return jax.shard_map(
        on_device if special else general_on_device,
        mesh=mesh,
        in_specs=placed,
        out_specs=P("arc", "par"),
        check_vma=False,
    )
```

```python
import math

import jax
import jax.numpy as jnp
from jax import lax
from jax.experimental import pallas as pl
from jax.experimental.pallas import tpu as pltpu
from jax.sharding import PartitionSpec as P


KERNEL_GAIN = 8.0


def mixing_matrices(epoch_index, whitening, epochs, row_scale):
    times_arc = epoch_index.astype(jnp.float32) / jnp.float32(4 * epochs - 1)
    later_time = times_arc[:, :, None]
    earlier_time = times_arc[:, None, :]
    green_part = jnp.minimum(later_time, earlier_time) * (
        1.0 - jnp.maximum(later_time, earlier_time)
    )
    kernel = jnp.eye(epochs, dtype=jnp.float32)[None] + KERNEL_GAIN / epochs * green_part
    mixing = jnp.einsum("acij,ajk->acik", whitening, kernel, precision=lax.Precision.HIGHEST)
    return mixing * row_scale


def gram_matrices(mixing):
    return jnp.einsum("acki,ackj->acij", mixing, mixing, precision=lax.Precision.HIGHEST)


def halves(value):
    high = lax.reduce_precision(value, 8, 7)
    return high.astype(jnp.bfloat16), (value - high).astype(jnp.bfloat16)


def mixed_rows(gram, rows):
    high, low = halves(gram)
    both = jnp.concatenate([high, low], axis=1)
    out = jnp.einsum("aij,ajn->ain", both, rows, preferred_element_type=jnp.float32)
    epochs = gram.shape[1]
    return halves(out[:, :epochs] + out[:, epochs:])


def product(rows, columns):
    contract = (((0, 1), (0, 1)), ((), ()))
    return sum(
        lax.dot_general(part, columns, contract, preferred_element_type=jnp.float32)
        for part in rows
    )


def general_on_device(partials, epoch_index, whitening):
    arc_local = partials.shape[0]
    epochs = epoch_index.shape[1]
    param_count = partials.shape[3]
    arc_count = lax.axis_size("arc")
    par_count = lax.axis_size("par")
    row_block = param_count // arc_count
    col_block = param_count // par_count
    row_scale = 1.0 / math.sqrt(3 * epochs * arc_local * arc_count)
    gram = gram_matrices(mixing_matrices(epoch_index, whitening, epochs, row_scale))
    gram = lax.all_gather(gram, "arc", axis=0, tiled=True)
    rows = lax.all_to_all(partials, "arc", split_axis=3, concat_axis=0, tiled=True)
    rows = lax.all_gather(rows, "par", axis=2, tiled=True)
    columns = lax.all_to_all(partials, "par", split_axis=3, concat_axis=2, tiled=True)
    columns = lax.all_gather(columns, "arc", axis=0, tiled=True)
    mixed = mixed_rows(gram.reshape(-1, epochs, epochs), rows.reshape(-1, epochs, row_block))
    return product(mixed, columns.reshape(-1, epochs, col_block))


def place(z, arrays, choose, blocks, share):
    width = arrays[0].shape[1] // blocks
    depth = sum(arrays[picks[0][1]].shape[0] for picks in choose)
    dtype = arrays[0].dtype

    def body(z_ref, *refs):
        out, part = refs[-2:]
        start = 0
        for picks in choose:
            size = refs[picks[0][1]].shape[0]
            for test, which in picks:

                @pl.when(test(z_ref[0]))
                def _(which=which, start=start, size=size):
                    for i in range(blocks):
                        out[i, start : start + size, :] = refs[which][:, i * width : (i + 1) * width]

            start += size
        for i in range(share):
            part[i] = out[z_ref[0] * share + i]

    vmem = pl.BlockSpec(memory_space=pltpu.VMEM)
    return pl.pallas_call(
        body,
        in_specs=[pl.BlockSpec(memory_space=pltpu.SMEM)] + [vmem] * len(arrays),
        out_specs=[vmem, vmem],
        out_shape=[
            jax.ShapeDtypeStruct((blocks, depth, width), dtype),
            jax.ShapeDtypeStruct((share, depth, width), dtype),
        ],
        cost_estimate=pl.CostEstimate(
            flops=0, bytes_accessed=4 * blocks * depth * width, transcendentals=0
        ),
        name="place",
    )(z.reshape(1), *arrays)


def update(total, slots, gram, component, rows, columns, steps=4):
    arcs, epochs = len(gram), gram[0].shape[-1]
    components = gram[0].shape[0]
    height = rows[0][0].shape[2]
    parts, _, width = columns[0][0][0].shape
    first = total is None
    sizes = [v.shape[1] if at is None else v.shape[1] // components for v, at in rows]
    count = len(rows)
    tile = height // steps
    depth = arcs * epochs

    def body(slot_ref, *refs):
        gram_refs, refs = refs[:arcs], refs[arcs:]
        row_refs, refs = refs[:count], refs[count:]
        col_refs, refs = refs[: count * arcs], refs[count * arcs :]
        out_ref, high_ref, low_ref, col_all = refs[-4:]
        n, m = pl.program_id(0), pl.program_id(1)

        @pl.when((n == 0) & (m == 0))
        def _():
            for slot in range(arcs):
                arc = slot_ref[slot]
                piece = jnp.concatenate([r[arc] for r in row_refs], axis=0)
                matrix = gram_refs[slot][0]
                high = matrix.astype(jnp.bfloat16)
                low = (matrix - high.astype(jnp.float32)).astype(jnp.bfloat16)
                both = jnp.concatenate([high, low], axis=0)
                contract = (((0,), (1,)), ((), ()))
                mixed = lax.dot_general(piece, both, contract, preferred_element_type=jnp.float32)
                mixed = mixed[:, :epochs] + mixed[:, epochs:]
                head = mixed.astype(jnp.bfloat16)
                at = slice(slot * epochs, (slot + 1) * epochs)
                high_ref[:, at] = head
                low_ref[:, at] = (mixed - head.astype(jnp.float32)).astype(jnp.bfloat16)

        @pl.when(m == 0)
        def _():
            for slot in range(arcs):
                start = slot * epochs
                for i, size in enumerate(sizes):
                    col_all[start : start + size, :] = col_refs[i * arcs + slot][0]
                    start += size

        span = pl.ds(pl.multiple_of(m * tile, tile), tile)
        value = jnp.dot(high_ref[span, :], col_all[...], preferred_element_type=jnp.float32)
        value = value + jnp.dot(low_ref[span, :], col_all[...], preferred_element_type=jnp.float32)
        if first:
            out_ref[...] = value
        else:
            out_ref[...] = refs[0][...] + value

    args = list(gram)
    in_specs = [pl.BlockSpec((1, epochs, epochs), lambda n, m, _: (component, 0, 0))] * arcs
    for (v, at), size in zip(rows, sizes):
        block = 0 if at is None else at
        args.append(v)
        in_specs.append(
            pl.BlockSpec((arcs, size, height), lambda n, m, _, block=block: (0, block, 0))
        )
    for (arrays, at), size in zip(columns, sizes):
        block = 0 if at is None else at
        args.extend(arrays)
        in_specs.extend(
            [pl.BlockSpec((1, size, width), lambda n, m, _, block=block: (n, block, 0))] * arcs
        )
    whole = pl.BlockSpec((tile, width), lambda n, m, _: (m, n))
    aliases = {}
    if not first:
        in_specs.append(whole)
        aliases = {len(args) + 1: 0}
        args.append(total)
    return pl.pallas_call(
        body,
        grid_spec=pltpu.PrefetchScalarGridSpec(
            num_scalar_prefetch=1,
            grid=(parts, steps),
            in_specs=in_specs,
            out_specs=whole,
            scratch_shapes=[
                pltpu.VMEM((height, depth), jnp.bfloat16),
                pltpu.VMEM((height, depth), jnp.bfloat16),
                pltpu.VMEM((depth, width), jnp.bfloat16),
            ],
        ),
        out_shape=jax.ShapeDtypeStruct((height, parts * width), jnp.float32),
        input_output_aliases=aliases,
        compiler_params=pltpu.CompilerParams(vmem_limit_bytes=24 * 1024 * 1024),
        cost_estimate=pl.CostEstimate(
            flops=4 * height * parts * width * depth,
            bytes_accessed=8 * height * parts * width,
            transcendentals=0,
        ),
        name="update",
    )(slots, *args)


def on_device(partials, epoch_index, whitening):
    arc_local, components, epoch_block, param_count = partials.shape
    epochs = epoch_index.shape[1]
    arc_count = lax.axis_size("arc")
    par_count = lax.axis_size("par")
    total_arcs = arc_local * arc_count
    row_scale = 1.0 / math.sqrt(3 * epochs * total_arcs)
    z = lax.axis_index("par")
    me = lax.axis_index("arc")
    bottom = z == 0
    top = z == par_count - 1

    first = jnp.where(bottom, 1, z - 1)
    second = jnp.where(bottom, 2, jnp.where(top, z - 2, z + 1))
    third = jnp.where(bottom, 3, jnp.where(top, z - 3, jnp.where(z == 1, 3, 0)))
    order = jnp.stack([z, first, second, third])
    mixing = mixing_matrices(epoch_index, whitening, epochs, row_scale)
    mixing = mixing.reshape(arc_local, components, epochs, par_count, epoch_block)
    mixing = jnp.take(mixing, order, axis=3).reshape(arc_local, components, epochs, epochs)
    gram = gram_matrices(mixing)[0]

    def hop(near, far, v):
        moves = [(i, i ^ (far if i % 2 else near)) for i in range(arc_count)]
        return lax.ppermute(v, "arc", moves)

    even, odd = [0, 2, 4, 6, 1, 5, 3, 7], [0, 4, 2, 6, 1, 3, 5, 7]
    slots = me ^ jnp.where(me % 2 == 1, jnp.array(odd), jnp.array(even))
    slots = slots.astype(jnp.int32)

    def in_plane(v):
        one = hop(2, 4, v)
        two = hop(4, 2, v)
        both = hop(4, 2, one)
        held = [v, one, two, both]
        return held + [hop(1, 1, w) for w in held]

    def exchange(blocks, part):
        rows = lax.all_to_all(blocks, "arc", split_axis=0, concat_axis=0, tiled=True)
        return rows, in_plane(part)

    def along(pairs, v):
        return lax.ppermute(v, "par", pairs)

    pick1 = [(lambda i: i == 0, 1), (lambda i: i > 0, 0)]
    pick2 = [
        (lambda i: i == 0, 3),
        (lambda i: i == 3, 2),
        (lambda i: (i == 1) | (i == 2), 1),
    ]
    pick3 = [
        (lambda i: i == 0, 5),
        (lambda i: i == 1, 3),
        (lambda i: i == 2, 2),
        (lambda i: i == 3, 4),
    ]
    share = arc_count // par_count

    own = partials.reshape(components * epoch_block, param_count)
    blocks, part = place(z, [own], [[(lambda i: i >= 0, 0)]], arc_count, share)
    own_rows, own_columns = exchange(blocks, part)
    grams = in_plane(gram)
    total = None
    for c in range(components):
        up = [own[c * epoch_block : (c + 1) * epoch_block]]
        down = list(up)
        for step in range(par_count - 1):
            pairs = [(i, i + 1) for i in range(step, par_count - 1)]
            up.append(along(pairs, up[-1]))
            pairs = [(par_count - 1 - i, par_count - 1 - j) for i, j in pairs]
            down.append(along(pairs, down[-1]))
        arrived = [v for both in zip(up[1:], down[1:]) for v in both]
        blocks, part = place(z, arrived, [pick1, pick2, pick3], arc_count, share)
        rows, columns = exchange(blocks, part)
        total = update(
            total, slots, grams, c, [(own_rows, c), (rows, None)],
            [(own_columns, c), (columns, None)],
        )
    return total


def solution(mesh):
    placed = (P("arc", None, "par", None), P("arc", None), P("arc", None, None, None))
    special = mesh.shape["par"] == 4 and mesh.shape["arc"] == 8

    def body(*args):
        return on_device(*args)

    return jax.shard_map(
        body if special else general_on_device,
        mesh=mesh,
        in_specs=placed,
        out_specs=P("arc", "par"),
        check_vma=False,
    )
```

```python
import math

import jax
import jax.numpy as jnp
from jax import lax
from jax.experimental import pallas as pl
from jax.experimental.pallas import tpu as pltpu
from jax.sharding import PartitionSpec as P


KERNEL_GAIN = 8.0


def mixing_matrices(epoch_index, whitening, epochs, row_scale):
    times_arc = epoch_index.astype(jnp.float32) / jnp.float32(4 * epochs - 1)
    later_time = times_arc[:, :, None]
    earlier_time = times_arc[:, None, :]
    green_part = jnp.minimum(later_time, earlier_time) * (
        1.0 - jnp.maximum(later_time, earlier_time)
    )
    kernel = jnp.eye(epochs, dtype=jnp.float32)[None] + KERNEL_GAIN / epochs * green_part
    mixing = jnp.einsum("acij,ajk->acik", whitening, kernel, precision=lax.Precision.HIGHEST)
    return mixing * row_scale


def gram_matrices(mixing):
    return jnp.einsum("acki,ackj->acij", mixing, mixing, precision=lax.Precision.HIGHEST)


def halves(value):
    high = lax.reduce_precision(value, 8, 7)
    return high.astype(jnp.bfloat16), (value - high).astype(jnp.bfloat16)


def mixed_rows(gram, rows):
    high, low = halves(gram)
    both = jnp.concatenate([high, low], axis=1)
    out = jnp.einsum("aij,ajn->ain", both, rows, preferred_element_type=jnp.float32)
    epochs = gram.shape[1]
    return halves(out[:, :epochs] + out[:, epochs:])


def product(rows, columns):
    contract = (((0, 1), (0, 1)), ((), ()))
    return sum(
        lax.dot_general(part, columns, contract, preferred_element_type=jnp.float32)
        for part in rows
    )


def general_on_device(partials, epoch_index, whitening):
    arc_local = partials.shape[0]
    epochs = epoch_index.shape[1]
    param_count = partials.shape[3]
    arc_count = lax.axis_size("arc")
    par_count = lax.axis_size("par")
    row_block = param_count // arc_count
    col_block = param_count // par_count
    row_scale = 1.0 / math.sqrt(3 * epochs * arc_local * arc_count)
    gram = gram_matrices(mixing_matrices(epoch_index, whitening, epochs, row_scale))
    gram = lax.all_gather(gram, "arc", axis=0, tiled=True)
    rows = lax.all_to_all(partials, "arc", split_axis=3, concat_axis=0, tiled=True)
    rows = lax.all_gather(rows, "par", axis=2, tiled=True)
    columns = lax.all_to_all(partials, "par", split_axis=3, concat_axis=2, tiled=True)
    columns = lax.all_gather(columns, "arc", axis=0, tiled=True)
    mixed = mixed_rows(gram.reshape(-1, epochs, epochs), rows.reshape(-1, epochs, row_block))
    return product(mixed, columns.reshape(-1, epochs, col_block))


def place(z, arrays, choose, blocks, share):
    width = arrays[0].shape[1] // blocks
    depth = sum(arrays[picks[0][1]].shape[0] for picks in choose)
    dtype = arrays[0].dtype

    def body(z_ref, *refs):
        out, part = refs[-2:]
        start = 0
        for picks in choose:
            size = refs[picks[0][1]].shape[0]
            for test, which in picks:

                @pl.when(test(z_ref[0]))
                def _(which=which, start=start, size=size):
                    for i in range(blocks):
                        out[i, start : start + size, :] = refs[which][:, i * width : (i + 1) * width]

            start += size
        for i in range(share):
            part[i] = out[z_ref[0] * share + i]

    vmem = pl.BlockSpec(memory_space=pltpu.VMEM)
    return pl.pallas_call(
        body,
        in_specs=[pl.BlockSpec(memory_space=pltpu.SMEM)] + [vmem] * len(arrays),
        out_specs=[vmem, vmem],
        out_shape=[
            jax.ShapeDtypeStruct((blocks, depth, width), dtype),
            jax.ShapeDtypeStruct((share, depth, width), dtype),
        ],
        cost_estimate=pl.CostEstimate(
            flops=0, bytes_accessed=4 * blocks * depth * width, transcendentals=0
        ),
        name="place",
    )(z.reshape(1), *arrays)


def place_own(z, block, gram, blocks, share):
    width = block.shape[1] // blocks
    depth = block.shape[0]
    count, epochs, _ = gram.shape
    rest = depth // count

    def body(z_ref, block_ref, gram_ref, out, part):
        for i in range(blocks):
            out[i] = block_ref[:, i * width : (i + 1) * width]
        for i in range(share):
            part[i] = out[z_ref[0] * share + i]
        for c in range(count):
            matrix = gram_ref[c]
            high = matrix.astype(jnp.bfloat16)
            low = (matrix - high.astype(jnp.float32)).astype(jnp.bfloat16)
            at = slice(c * rest, (c + 1) * rest)
            for half, value in enumerate((high, low)):
                for q in range(epochs // rest):
                    lane = (half * (epochs // rest) + q) * epochs
                    part[share, at, lane : lane + epochs] = value[q * rest : (q + 1) * rest]

    vmem = pl.BlockSpec(memory_space=pltpu.VMEM)
    return pl.pallas_call(
        body,
        in_specs=[pl.BlockSpec(memory_space=pltpu.SMEM), vmem, vmem],
        out_specs=[vmem, vmem],
        out_shape=[
            jax.ShapeDtypeStruct((blocks, depth, width), block.dtype),
            jax.ShapeDtypeStruct((share + 1, depth, width), block.dtype),
        ],
        cost_estimate=pl.CostEstimate(
            flops=0, bytes_accessed=4 * blocks * depth * width, transcendentals=0
        ),
        name="place_own",
    )(z.reshape(1), block, gram)


def update(total, slots, components, epochs, work, steps=2):
    gram = work[0][2][0][0]
    arcs = len(gram)
    height = work[0][1][0][0].shape[2]
    _, whole_depth, width = gram[0].shape
    parts = work[0][2][1][0][0].shape[0]
    rest = whole_depth // components
    first = total is None
    sizes = [
        v.shape[1] if at is None else v.shape[1] // components for v, at in work[0][1]
    ]
    count = len(sizes)
    tile = height // steps
    depth = arcs * epochs
    whole_k = depth * len(work)

    def body(slot_ref, *refs):
        gram_refs, refs = refs[:arcs], refs[arcs:]
        row_refs, refs = refs[: count * len(work)], refs[count * len(work) :]
        col_refs, refs = refs[: count * arcs * len(work)], refs[count * arcs * len(work) :]
        out_ref, mixed_ref, col_all = refs[-3:]
        n, m = pl.program_id(0), pl.program_id(1)

        @pl.when((n == 0) & (m == 0))
        def _():
            for index in range(len(work)):
                for slot in range(arcs):
                    arc = slot_ref[slot]
                    own = row_refs[index * count : (index + 1) * count]
                    piece = jnp.concatenate([r[arc] for r in own], axis=0)
                    both = [
                        gram_refs[slot][0, :, q * epochs : (q + 1) * epochs]
                        for q in range(2 * epochs // rest)
                    ]
                    both = jnp.concatenate(both, axis=0)
                    contract = (((0,), (1,)), ((), ()))
                    mixed = lax.dot_general(
                        piece, both, contract, preferred_element_type=jnp.float32
                    )
                    mixed = mixed[:, :epochs] + mixed[:, epochs:]
                    head = mixed.astype(jnp.bfloat16)
                    tail = (mixed - head.astype(jnp.float32)).astype(jnp.bfloat16)
                    start = index * depth + slot * epochs
                    for t in range(steps):
                        span = slice(t * tile, (t + 1) * tile)
                        mixed_ref[t, :tile, start : start + epochs] = head[span]
                        mixed_ref[t, tile:, start : start + epochs] = tail[span]

        @pl.when(m == 0)
        def _():
            for index in range(len(work)):
                for slot in range(arcs):
                    start = index * depth + slot * epochs
                    for i, size in enumerate(sizes):
                        piece = col_refs[(index * count + i) * arcs + slot]
                        col_all[start : start + size, :] = piece[0]
                        start += size

        value = jnp.dot(mixed_ref[m], col_all[...], preferred_element_type=jnp.float32)
        value = value[:tile] + value[tile:]
        if first:
            out_ref[...] = value
        else:
            out_ref[...] = refs[0][...] + value

    args = list(gram)
    place_at = work[0][0]
    in_specs = [pl.BlockSpec((1, rest, width), lambda n, m, _: (parts, place_at, 0))] * arcs
    for _, rows, _ in work:
        for (v, at), size in zip(rows, sizes):
            block = 0 if at is None else at
            args.append(v)
            in_specs.append(
                pl.BlockSpec((arcs, size, height), lambda n, m, _, block=block: (0, block, 0))
            )
    for _, _, columns in work:
        for (arrays, at), size in zip(columns, sizes):
            block = 0 if at is None else at
            args.extend(arrays)
            in_specs.extend(
                [pl.BlockSpec((1, size, width), lambda n, m, _, block=block: (n, block, 0))] * arcs
            )
    args = [pltpu.with_memory_space_constraint(v, pltpu.HBM) for v in args]
    whole = pl.BlockSpec((tile, width), lambda n, m, _: (m, n))
    aliases = {}
    if not first:
        in_specs.append(whole)
        aliases = {len(args) + 1: 0}
        args.append(total)
    return pl.pallas_call(
        body,
        grid_spec=pltpu.PrefetchScalarGridSpec(
            num_scalar_prefetch=1,
            grid=(parts, steps),
            in_specs=in_specs,
            out_specs=whole,
            scratch_shapes=[
                pltpu.VMEM((steps, 2 * tile, whole_k), jnp.bfloat16),
                pltpu.VMEM((whole_k, width), jnp.bfloat16),
            ],
        ),
        out_shape=jax.ShapeDtypeStruct((height, parts * width), jnp.float32),
        input_output_aliases=aliases,
        compiler_params=pltpu.CompilerParams(
            vmem_limit_bytes=32 * 1024 * 1024
        ),
        cost_estimate=pl.CostEstimate(
            flops=4 * height * parts * width * whole_k,
            bytes_accessed=8 * height * parts * width,
            transcendentals=0,
        ),
        name="update",
    )(slots, *args)


def on_device(partials, epoch_index, whitening):
    arc_local, components, epoch_block, param_count = partials.shape
    epochs = epoch_index.shape[1]
    arc_count = lax.axis_size("arc")
    par_count = lax.axis_size("par")
    total_arcs = arc_local * arc_count
    row_scale = 1.0 / math.sqrt(3 * epochs * total_arcs)
    z = lax.axis_index("par")
    me = lax.axis_index("arc")
    bottom = z == 0
    top = z == par_count - 1

    first = jnp.where(bottom, 1, z - 1)
    second = jnp.where(bottom, 2, jnp.where(top, z - 2, z + 1))
    third = jnp.where(bottom, 3, jnp.where(top, z - 3, jnp.where(z == 1, 3, 0)))
    order = jnp.stack([z, first, second, third])
    mixing = mixing_matrices(epoch_index, whitening, epochs, row_scale)
    mixing = mixing.reshape(arc_local, components, epochs, par_count, epoch_block)
    mixing = jnp.take(mixing, order, axis=3).reshape(arc_local, components, epochs, epochs)
    gram = gram_matrices(mixing)[0]

    def hop(near, far, v):
        moves = [(i, i ^ (far if i % 2 else near)) for i in range(arc_count)]
        return lax.ppermute(v, "arc", moves)

    even, odd = [0, 2, 4, 6, 1, 5, 3, 7], [0, 4, 2, 6, 1, 3, 5, 7]
    slots = me ^ jnp.where(me % 2 == 1, jnp.array(odd), jnp.array(even))
    slots = slots.astype(jnp.int32)

    def in_plane(v):
        one = hop(2, 4, v)
        two = hop(4, 2, v)
        both = hop(4, 2, one)
        held = [v, one, two, both]
        return held + [hop(1, 1, w) for w in held]

    def exchange(blocks, part):
        rows = lax.all_to_all(blocks, "arc", split_axis=0, concat_axis=0, tiled=True)
        return rows, in_plane(part)

    def along(pairs, v):
        return lax.ppermute(v, "par", pairs)

    pick1 = [(lambda i: i == 0, 1), (lambda i: i > 0, 0)]
    pick2 = [
        (lambda i: i == 0, 3),
        (lambda i: i == 3, 2),
        (lambda i: (i == 1) | (i == 2), 1),
    ]
    pick3 = [
        (lambda i: i == 0, 5),
        (lambda i: i == 1, 3),
        (lambda i: i == 2, 2),
        (lambda i: i == 3, 4),
    ]
    share = arc_count // par_count

    own = partials.reshape(components * epoch_block, param_count)
    blocks, part = place_own(z, own, gram, arc_count, share)
    own_rows, own_columns = exchange(blocks, part)
    total = None
    for c in range(components):
        up = [own[c * epoch_block : (c + 1) * epoch_block]]
        down = list(up)
        for step in range(par_count - 1):
            pairs = [(i, i + 1) for i in range(step, par_count - 1)]
            up.append(along(pairs, up[-1]))
            pairs = [(par_count - 1 - i, par_count - 1 - j) for i, j in pairs]
            down.append(along(pairs, down[-1]))
        arrived = [v for both in zip(up[1:], down[1:]) for v in both]
        stages = [(arrived, [pick1, pick2, pick3])]
        rows, columns = [(own_rows, c)], [(own_columns, c)]
        for arrays, picks in stages:
            blocks, part = place(z, arrays, picks, arc_count, share)
            new_rows, new_columns = exchange(blocks, part)
            rows.append((new_rows, None))
            columns.append((new_columns, None))
        total = update(total, slots, components, epochs, [(c, rows, columns)])
    return total


def solution(mesh):
    placed = (P("arc", None, "par", None), P("arc", None), P("arc", None, None, None))
    special = mesh.shape["par"] == 4 and mesh.shape["arc"] == 8

    def body(*args):
        return on_device(*args)

    return jax.shard_map(
        body if special else general_on_device,
        mesh=mesh,
        in_specs=placed,
        out_specs=P("arc", "par"),
        check_vma=False,
    )
```

```python
import math

import jax
import jax.numpy as jnp
from jax import lax
from jax.experimental import pallas as pl
from jax.experimental.pallas import tpu as pltpu
from jax.sharding import PartitionSpec as P


KERNEL_GAIN = 8.0


def mixing_matrices(epoch_index, whitening, epochs, row_scale):
    times_arc = epoch_index.astype(jnp.float32) / jnp.float32(4 * epochs - 1)
    later_time = times_arc[:, :, None]
    earlier_time = times_arc[:, None, :]
    green_part = jnp.minimum(later_time, earlier_time) * (
        1.0 - jnp.maximum(later_time, earlier_time)
    )
    kernel = jnp.eye(epochs, dtype=jnp.float32)[None] + KERNEL_GAIN / epochs * green_part
    mixing = jnp.einsum("acij,ajk->acik", whitening, kernel, precision=lax.Precision.HIGHEST)
    return mixing * row_scale


def gram_matrices(mixing):
    return jnp.einsum("acki,ackj->acij", mixing, mixing, precision=lax.Precision.HIGHEST)


def halves(value):
    high = lax.reduce_precision(value, 8, 7)
    return high.astype(jnp.bfloat16), (value - high).astype(jnp.bfloat16)


def mixed_rows(gram, rows):
    high, low = halves(gram)
    both = jnp.concatenate([high, low], axis=1)
    out = jnp.einsum("aij,ajn->ain", both, rows, preferred_element_type=jnp.float32)
    epochs = gram.shape[1]
    return halves(out[:, :epochs] + out[:, epochs:])


def product(rows, columns):
    contract = (((0, 1), (0, 1)), ((), ()))
    return sum(
        lax.dot_general(part, columns, contract, preferred_element_type=jnp.float32)
        for part in rows
    )


def general_on_device(partials, epoch_index, whitening):
    arc_local = partials.shape[0]
    epochs = epoch_index.shape[1]
    param_count = partials.shape[3]
    arc_count = lax.axis_size("arc")
    par_count = lax.axis_size("par")
    row_block = param_count // arc_count
    col_block = param_count // par_count
    row_scale = 1.0 / math.sqrt(3 * epochs * arc_local * arc_count)
    gram = gram_matrices(mixing_matrices(epoch_index, whitening, epochs, row_scale))
    gram = lax.all_gather(gram, "arc", axis=0, tiled=True)
    rows = lax.all_to_all(partials, "arc", split_axis=3, concat_axis=0, tiled=True)
    rows = lax.all_gather(rows, "par", axis=2, tiled=True)
    columns = lax.all_to_all(partials, "par", split_axis=3, concat_axis=2, tiled=True)
    columns = lax.all_gather(columns, "arc", axis=0, tiled=True)
    mixed = mixed_rows(gram.reshape(-1, epochs, epochs), rows.reshape(-1, epochs, row_block))
    return product(mixed, columns.reshape(-1, epochs, col_block))


def place(z, arrays, choose, blocks, share):
    width = arrays[0].shape[1] // blocks
    depth = sum(arrays[picks[0][1]].shape[0] for picks in choose)
    dtype = arrays[0].dtype

    def body(z_ref, *refs):
        out, part = refs[-2:]
        start = 0
        for picks in choose:
            size = refs[picks[0][1]].shape[0]
            for test, which in picks:

                @pl.when(test(z_ref[0]))
                def _(which=which, start=start, size=size):
                    for i in range(blocks):
                        out[i, start : start + size, :] = refs[which][:, i * width : (i + 1) * width]

            start += size
        for i in range(share):
            part[i] = out[z_ref[0] * share + i]

    vmem = pl.BlockSpec(memory_space=pltpu.VMEM)
    return pl.pallas_call(
        body,
        in_specs=[pl.BlockSpec(memory_space=pltpu.SMEM)] + [vmem] * len(arrays),
        out_specs=[vmem, vmem],
        out_shape=[
            jax.ShapeDtypeStruct((blocks, depth, width), dtype),
            jax.ShapeDtypeStruct((share, depth, width), dtype),
        ],
        cost_estimate=pl.CostEstimate(
            flops=0, bytes_accessed=4 * blocks * depth * width, transcendentals=0
        ),
        name="place",
    )(z.reshape(1), *arrays)


def place_own(z, block, gram, blocks, share):
    width = block.shape[1] // blocks
    depth = block.shape[0]
    count, epochs, _ = gram.shape
    rest = depth // count

    def body(z_ref, block_ref, gram_ref, out, part):
        for i in range(blocks):
            out[i] = block_ref[:, i * width : (i + 1) * width]
        for i in range(share):
            part[i] = out[z_ref[0] * share + i]
        for c in range(count):
            matrix = gram_ref[c]
            high = matrix.astype(jnp.bfloat16)
            low = (matrix - high.astype(jnp.float32)).astype(jnp.bfloat16)
            at = slice(c * rest, (c + 1) * rest)
            for half, value in enumerate((high, low)):
                for q in range(epochs // rest):
                    lane = (half * (epochs // rest) + q) * epochs
                    part[share, at, lane : lane + epochs] = value[q * rest : (q + 1) * rest]

    vmem = pl.BlockSpec(memory_space=pltpu.VMEM)
    return pl.pallas_call(
        body,
        in_specs=[pl.BlockSpec(memory_space=pltpu.SMEM), vmem, vmem],
        out_specs=[vmem, vmem],
        out_shape=[
            jax.ShapeDtypeStruct((blocks, depth, width), block.dtype),
            jax.ShapeDtypeStruct((share + 1, depth, width), block.dtype),
        ],
        cost_estimate=pl.CostEstimate(
            flops=0, bytes_accessed=4 * blocks * depth * width, transcendentals=0
        ),
        name="place_own",
    )(z.reshape(1), block, gram)


def update(total, slots, components, epochs, work, steps=4):
    gram = work[0][2][0][0]
    arcs = len(gram)
    height = work[0][1][0][0].shape[2]
    _, whole_depth, width = gram[0].shape
    parts = work[0][2][1][0][0].shape[0]
    rest = whole_depth // components
    first = total is None
    sizes = [
        v.shape[1] if at is None else v.shape[1] // components for v, at in work[0][1]
    ]
    count = len(sizes)
    tile = height // steps
    depth = arcs * epochs
    whole_k = depth * len(work)

    def body(slot_ref, *refs):
        gram_refs, refs = refs[:arcs], refs[arcs:]
        row_refs, refs = refs[: count * len(work)], refs[count * len(work) :]
        col_refs, refs = refs[: count * arcs * len(work)], refs[count * arcs * len(work) :]
        out_ref, mixed_ref, col_all = refs[-3:]
        n, m = pl.program_id(0), pl.program_id(1)

        @pl.when((n == 0) & (m == 0))
        def _():
            for index in range(len(work)):
                for slot in range(arcs):
                    arc = slot_ref[slot]
                    own = row_refs[index * count : (index + 1) * count]
                    piece = jnp.concatenate([r[arc] for r in own], axis=0)
                    both = [
                        gram_refs[slot][0, :, q * epochs : (q + 1) * epochs]
                        for q in range(2 * epochs // rest)
                    ]
                    both = jnp.concatenate(both, axis=0)
                    contract = (((0,), (1,)), ((), ()))
                    mixed = lax.dot_general(
                        piece, both, contract, preferred_element_type=jnp.float32
                    )
                    mixed = mixed[:, :epochs] + mixed[:, epochs:]
                    head = mixed.astype(jnp.bfloat16)
                    tail = (mixed - head.astype(jnp.float32)).astype(jnp.bfloat16)
                    start = index * depth + slot * epochs
                    for t in range(steps):
                        span = slice(t * tile, (t + 1) * tile)
                        mixed_ref[t, :tile, start : start + epochs] = head[span]
                        mixed_ref[t, tile:, start : start + epochs] = tail[span]

        @pl.when(m == 0)
        def _():
            for index in range(len(work)):
                for slot in range(arcs):
                    start = index * depth + slot * epochs
                    for i, size in enumerate(sizes):
                        piece = col_refs[(index * count + i) * arcs + slot]
                        col_all[start : start + size, :] = piece[0]
                        start += size

        value = jnp.dot(mixed_ref[m], col_all[...], preferred_element_type=jnp.float32)
        value = value[:tile] + value[tile:]
        if first:
            out_ref[...] = value
        else:
            out_ref[...] = refs[0][...] + value

    args = list(gram)
    place_at = work[0][0]
    in_specs = [pl.BlockSpec((1, rest, width), lambda n, m, _: (parts, place_at, 0))] * arcs
    for _, rows, _ in work:
        for (v, at), size in zip(rows, sizes):
            block = 0 if at is None else at
            args.append(v)
            in_specs.append(
                pl.BlockSpec((arcs, size, height), lambda n, m, _, block=block: (0, block, 0))
            )
    for _, _, columns in work:
        for (arrays, at), size in zip(columns, sizes):
            block = 0 if at is None else at
            args.extend(arrays)
            in_specs.extend(
                [pl.BlockSpec((1, size, width), lambda n, m, _, block=block: (n, block, 0))] * arcs
            )
    moved = {id(v) for _, rows, _ in work for v, _ in rows}
    args = [
        v if id(v) in moved else pltpu.with_memory_space_constraint(v, pltpu.HBM) for v in args
    ]
    whole = pl.BlockSpec((tile, width), lambda n, m, _: (m, n))
    aliases = {}
    if not first:
        in_specs.append(whole)
        aliases = {len(args) + 1: 0}
        args.append(total)
    return pl.pallas_call(
        body,
        grid_spec=pltpu.PrefetchScalarGridSpec(
            num_scalar_prefetch=1,
            grid=(parts, steps),
            in_specs=in_specs,
            out_specs=whole,
            scratch_shapes=[
                pltpu.VMEM((steps, 2 * tile, whole_k), jnp.bfloat16),
                pltpu.VMEM((whole_k, width), jnp.bfloat16),
            ],
        ),
        out_shape=jax.ShapeDtypeStruct((height, parts * width), jnp.float32),
        input_output_aliases=aliases,
        compiler_params=pltpu.CompilerParams(
            vmem_limit_bytes=32 * 1024 * 1024
        ),
        cost_estimate=pl.CostEstimate(
            flops=4 * height * parts * width * whole_k,
            bytes_accessed=8 * height * parts * width,
            transcendentals=0,
        ),
        name="update",
    )(slots, *args)


def on_device(partials, epoch_index, whitening):
    arc_local, components, epoch_block, param_count = partials.shape
    epochs = epoch_index.shape[1]
    arc_count = lax.axis_size("arc")
    par_count = lax.axis_size("par")
    total_arcs = arc_local * arc_count
    row_scale = 1.0 / math.sqrt(3 * epochs * total_arcs)
    z = lax.axis_index("par")
    me = lax.axis_index("arc")
    bottom = z == 0
    top = z == par_count - 1

    first = jnp.where(bottom, 1, z - 1)
    second = jnp.where(bottom, 2, jnp.where(top, z - 2, z + 1))
    third = jnp.where(bottom, 3, jnp.where(top, z - 3, jnp.where(z == 1, 3, 0)))
    order = jnp.stack([z, first, second, third])
    mixing = mixing_matrices(epoch_index, whitening, epochs, row_scale)
    mixing = mixing.reshape(arc_local, components, epochs, par_count, epoch_block)
    mixing = jnp.take(mixing, order, axis=3).reshape(arc_local, components, epochs, epochs)
    gram = gram_matrices(mixing)[0]

    def hop(near, far, v):
        moves = [(i, i ^ (far if i % 2 else near)) for i in range(arc_count)]
        return lax.ppermute(v, "arc", moves)

    even, odd = [0, 2, 4, 6, 1, 5, 3, 7], [0, 4, 2, 6, 1, 3, 5, 7]
    slots = me ^ jnp.where(me % 2 == 1, jnp.array(odd), jnp.array(even))
    slots = slots.astype(jnp.int32)

    def in_plane(v):
        one = hop(2, 4, v)
        two = hop(4, 2, v)
        both = hop(4, 2, one)
        held = [v, one, two, both]
        return held + [hop(1, 1, w) for w in held]

    def exchange(blocks, part):
        rows = lax.all_to_all(blocks, "arc", split_axis=0, concat_axis=0, tiled=True)
        return rows, in_plane(part)

    def along(pairs, v):
        return lax.ppermute(v, "par", pairs)

    pick1 = [(lambda i: i == 0, 1), (lambda i: i > 0, 0)]
    pick2 = [
        (lambda i: i == 0, 3),
        (lambda i: i == 3, 2),
        (lambda i: (i == 1) | (i == 2), 1),
    ]
    pick3 = [
        (lambda i: i == 0, 5),
        (lambda i: i == 1, 3),
        (lambda i: i == 2, 2),
        (lambda i: i == 3, 4),
    ]
    share = arc_count // par_count

    own = partials.reshape(components * epoch_block, param_count)
    blocks, part = place_own(z, own, gram, arc_count, share)
    total = None
    behind, blocks = lax.optimization_barrier((own, blocks))
    own_rows, own_columns = exchange(blocks, part)
    for c in range(components):
        up = [(behind if c else own)[c * epoch_block : (c + 1) * epoch_block]]
        down = list(up)
        for step in range(par_count - 1):
            pairs = [(i, i + 1) for i in range(step, par_count - 1)]
            up.append(along(pairs, up[-1]))
            pairs = [(par_count - 1 - i, par_count - 1 - j) for i, j in pairs]
            down.append(along(pairs, down[-1]))
        arrived = [v for both in zip(up[1:], down[1:]) for v in both]
        stages = [(arrived, [pick1, pick2, pick3])]
        rows, columns = [(own_rows, c)], [(own_columns, c)]
        for arrays, picks in stages:
            blocks, part = place(z, arrays, picks, arc_count, share)
            new_rows, new_columns = exchange(blocks, part)
            rows.append((new_rows, None))
            columns.append((new_columns, None))
        total = update(total, slots, components, epochs, [(c, rows, columns)])
    return total


def solution(mesh):
    placed = (P("arc", None, "par", None), P("arc", None), P("arc", None, None, None))
    special = mesh.shape["par"] == 4 and mesh.shape["arc"] == 8

    def body(*args):
        return on_device(*args)

    return jax.shard_map(
        body if special else general_on_device,
        mesh=mesh,
        in_specs=placed,
        out_specs=P("arc", "par"),
        check_vma=False,
    )
```
